32 devices in a mesh: groups: 2 (over x), span: 16 (over z, y, core).
Axes of the slice: x: 2, y: 2, z: 4, core: 2. Of those that a mesh axis runs over, the one named last changes fastest.
Arguments:
- queries: bfloat16 [8192, 2560], P(('groups', 'span')), parts along dimension 0, may hold values from -100 to 100
- cross_queries: bfloat16 [8192, 2560], P(('groups', 'span')), parts along dimension 0, may hold values from -100 to 100
- frame_kv: bfloat16 [8192, 5120], P(('groups', 'span')), parts along dimension 0, may hold values from -7 to 7
- sink_kv: bfloat16 [32, 64, 5120], P(('groups', 'span')), parts along dimension 0, may hold values from -5 to 5
- prompt_kv: bfloat16 [4, 512, 5120], P('groups', 'span'), parts along dimension 0, may hold values from -7 to 7
- switch: int32 [8], P('groups'), parts along dimension 0, may hold values from 0 to 4
Outputs:
- self_out: bfloat16 [8192, 2560], P(('groups', 'span')), parts along dimension 0
- cross_out: bfloat16 [8192, 2560], P(('groups', 'span')), parts along dimension 0
The draws below stay inside these ranges and needn't reach their ends.
There are 2 independent parts, one for each index of `groups`. The reference program is written for one: setup_inputs(seed, part) draws one part's arguments, and reference() takes and returns one part's arrays. A program takes and returns all parts, laid end to end along the dimension named above; each array names one. Nothing has to cross between parts.
All inputs are finite; a program needn't handle non-finite values.
Results may differ from the reference program's by a relative error of at most 0.006.
Values may be sent and summed in bfloat16 or wider, within the bound.
A program may use at most 128 MiB of HBM per device.

```python
import math
import jax
import jax.numpy as jnp
from jax import lax

HEADS = 20
HDIM = 128
FRAME = 256
WIN = 4
PTOK = 512
PROMPTS = 2
HD = 2560
STREAMS = 4
TOKENS = 4096
N_SPAN = 16


def clipped_normal(key, shape):
    return jnp.clip(jax.random.normal(key, shape, jnp.float32), -5.0, 5.0)


def frame_keys(key):
    key_rows = clipped_normal(jax.random.fold_in(key, 7), (TOKENS, HEADS * HDIM))
    return key_rows


def draw_frame_kv(key, part):
    values = clipped_normal(jax.random.fold_in(key, 8), (TOKENS, HEADS * HDIM))
    return jnp.concatenate([frame_keys(key), values], axis=1).astype(jnp.bfloat16)


def draw_queries(key, part):
    query_rows = clipped_normal(jax.random.fold_in(key, 9), (TOKENS, HEADS * HDIM))
    return query_rows.astype(jnp.bfloat16)


def draw_prompt_kv(key, part):
    stacked = []
    for prompt in range(PROMPTS):
        key_rows = clipped_normal(jax.random.fold_in(key, 20 + prompt), (PTOK, HEADS * HDIM))
        values = clipped_normal(jax.random.fold_in(key, 40 + prompt), (PTOK, HEADS * HDIM))
        stacked.append(jnp.concatenate([key_rows, values], axis=1))
    return jnp.stack(stacked, axis=0).astype(jnp.bfloat16)


def draw_cross_queries(key, part):
    query_rows = clipped_normal(jax.random.fold_in(key, 13), (TOKENS, HEADS * HDIM))
    return query_rows.astype(jnp.bfloat16)


def place_ends(entries, stream_key, smallest, largest):
    spot = [jax.random.randint(jax.random.fold_in(stream_key, axis), (), 0, length) for axis, length in enumerate(entries.shape)]
    longest = entries.shape.index(max(entries.shape))
    neighbour = spot[:longest] + [(spot[longest] + 1) % entries.shape[longest]] + spot[longest + 1:]
    return entries.at[tuple(spot)].set(smallest).at[tuple(neighbour)].set(largest)


def shard_levels(own_key, extent, cuts, smallest, high):
    loudness, own = 1.0, jax.random.fold_in(own_key, 6)
    for axis_at, shards_of in cuts:
        steps = jnp.exp(jax.random.uniform(jax.random.fold_in(own, axis_at), (shards_of,), jnp.float32, smallest / len(cuts), high / len(cuts)))
        loudness = loudness * jnp.repeat(steps, extent[axis_at] // shards_of).reshape([-1 if axis == axis_at else 1 for axis in range(len(extent))])
    return loudness


def scatter_about(rng, dims, spread, most, pieces=(), held_as=jnp.bfloat16):
    level = shard_levels(rng, dims, pieces, -0.22, 0.18) if pieces else 1.0
    result = jax.random.normal(rng, dims, jnp.float32) * spread * level
    return jnp.minimum(jnp.maximum(result, -most), most).astype(held_as)


def setup_inputs(seed: int = 0, part: int = 0) -> dict:
    keys = jax.random.split(jax.random.key(seed), 7)
    part_keys = jax.random.split(jax.random.fold_in(keys[6], part), 7)
    return {
        "queries": draw_queries(jax.random.fold_in(jax.random.fold_in(keys[6], part), 71), part),
        "cross_queries": draw_cross_queries(jax.random.fold_in(jax.random.fold_in(keys[6], part), 71), part),
        "frame_kv": draw_frame_kv(jax.random.fold_in(jax.random.fold_in(keys[6], part), 71), part),
        "sink_kv": scatter_about(part_keys[3], (N_SPAN, FRAME // WIN, 2 * HD), 1.0, 5.0, ((0, 16),)),
        "prompt_kv": draw_prompt_kv(jax.random.fold_in(jax.random.fold_in(keys[6], part), 71), part),
        "switch": place_ends(jax.random.randint(part_keys[5], (STREAMS,), 0, WIN + 1), jax.random.fold_in(part_keys[5], 1), 0, WIN).astype(jnp.int32),
    }


def softmax_blend(query_rows, key_rows, value_rows, visible):
    scores = jnp.einsum('qhd,khd->hqk', query_rows, key_rows) * (1.0 / math.sqrt(HDIM))
    if visible is not None:
        scores = jnp.where(visible[None], scores, -jnp.inf)
    row_max = lax.optimization_barrier(jnp.max(scores, axis=-1, keepdims=True))
    weights = jnp.exp(scores - row_max)
    totals = lax.optimization_barrier(jnp.sum(weights, axis=-1))
    rounded = lax.optimization_barrier(weights.astype(jnp.bfloat16)).astype(jnp.float32)
    blended = jnp.einsum('hqk,khd->qhd', rounded, value_rows)
    return (blended / jnp.transpose(totals)[:, :, None]).astype(jnp.bfloat16)

def reference(queries, cross_queries, frame_kv, sink_kv, prompt_kv, switch):
    streams = N_SPAN // WIN
    stream_queries = jnp.transpose(queries.astype(jnp.float32).reshape(WIN, streams, FRAME, HEADS, HDIM), (1, 0, 2, 3, 4)).reshape(streams, WIN * FRAME, HEADS, HDIM)
    stream_kv = jnp.transpose(frame_kv.astype(jnp.float32).reshape(WIN, streams, FRAME, 2, HEADS, HDIM), (1, 0, 2, 3, 4, 5)).reshape(streams, WIN * FRAME, 2, HEADS, HDIM)
    stream_sink = jnp.transpose(sink_kv.astype(jnp.float32).reshape(WIN, streams, FRAME // WIN, 2, HEADS, HDIM), (1, 0, 2, 3, 4, 5)).reshape(streams, FRAME, 2, HEADS, HDIM)
    key_block = jnp.concatenate([jnp.zeros((FRAME,), jnp.int32), jnp.repeat(jnp.arange(WIN, dtype=jnp.int32) + 1, FRAME)])
    query_frame = jnp.repeat(jnp.arange(WIN, dtype=jnp.int32), FRAME)
    visible = key_block[None, :] <= query_frame[:, None] + 1

    def one_stream(inputs_one):
        query_rows, kv_rows, sink_rows = inputs_one
        key_rows = jnp.concatenate([sink_rows[:, 0], kv_rows[:, 0]], axis=0)
        value_rows = jnp.concatenate([sink_rows[:, 1], kv_rows[:, 1]], axis=0)
        return softmax_blend(query_rows, key_rows, value_rows, visible).reshape(WIN * FRAME, HEADS * HDIM)
    per_stream = lax.map(one_stream, (stream_queries, stream_kv, stream_sink))
    self_out = jnp.transpose(per_stream.reshape(streams, WIN, FRAME, HEADS * HDIM), (1, 0, 2, 3)).reshape(N_SPAN * FRAME, HEADS * HDIM)
    devices = jnp.arange(N_SPAN, dtype=jnp.int32)
    window_place = devices // streams
    stream_index = devices % streams
    prompt_id = (window_place >= switch[stream_index]).astype(jnp.int32)
    frame_queries = cross_queries.astype(jnp.float32).reshape(N_SPAN, FRAME, HEADS, HDIM)
    bank = prompt_kv.astype(jnp.float32).reshape(PROMPTS, PTOK, 2, HEADS, HDIM)

    def one_frame(inputs_one):
        query_rows, chosen = inputs_one
        picked = lax.dynamic_index_in_dim(bank, chosen.astype(jnp.int32), 0, keepdims=False)
        return softmax_blend(query_rows, picked[:, 0], picked[:, 1], None).reshape(FRAME, HEADS * HDIM)
    cross_out = lax.map(one_frame, (frame_queries, prompt_id)).reshape(N_SPAN * FRAME, HEADS * HDIM)
    return (self_out, cross_out)
```

```python
import functools
import math

import jax
import jax.numpy as jnp
from jax import lax
from jax.experimental import pallas as pl
from jax.experimental.pallas import tpu as pltpu
from jax.sharding import PartitionSpec as P

HEADS = 20
HDIM = 128
WIN = 4
BUNDLE = 4
CHUNKS = HEADS // BUNDLE
BW = BUNDLE * HDIM
WIDTH = HEADS * HDIM
SCALE = 1.0 / math.sqrt(HDIM)
LOG2E = 1.4426950408889634
MESH = pl.DeviceIdType.MESH


def attend(query, pieces):
    scores = [
        lax.dot_general(query, keys, (((1,), (1,)), ((), ())), preferred_element_type=jnp.float32)
        for keys, _ in pieces
    ]
    peak = functools.reduce(
        jnp.maximum, [jnp.max(piece, axis=1, keepdims=True) for piece in scores]
    )
    total, blended = None, None
    for piece, (_, values) in zip(scores, pieces):
        weights = jnp.exp2((piece - peak) * (SCALE * LOG2E))
        part_sum = jnp.sum(weights, axis=1, keepdims=True)
        part = jnp.dot(weights.astype(jnp.bfloat16), values, preferred_element_type=jnp.float32)
        total = part_sum if total is None else total + part_sum
        blended = part if blended is None else blended + part
    return blended / total, peak * (SCALE * LOG2E), total


def cols(chunk, width=BW, base=0):
    return pl.ds(pl.multiple_of(base + chunk * width, 128), width)


def head_cols(head, base=0):
    return pl.ds(pl.multiple_of(base + head * HDIM, 128), HDIM)


def self_kernel(
    q_ref, kv_ref, sink_ref, out_ref,
    kv_prev, sinks, q_in, o_send, o_recv, st_send, st_recv,
    kv_s, kv_r, q_s, q_r, s_s, s_r, o_s, o_r, st_s, st_r,
):
    stride = lax.axis_size("span") // WIN
    me = lax.axis_index("span")
    place = me // stride
    stream = me % stride
    rows_s = sink_ref.shape[0]

    def at_place(index):
        return {"span": index * stride + stream}

    def remote(src, dst, send, recv, index):
        return pltpu.make_async_remote_copy(
            src_ref=src, dst_ref=dst, send_sem=send, recv_sem=recv,
            device_id=at_place(index), device_id_type=MESH,
        )

    def kv_copies(chunk):
        pairs = []
        for part in range(2):
            where = cols(chunk, BW, part * WIDTH)
            pairs.append((kv_ref.at[:, where], kv_prev.at[:, where]))
        for part in range(2):
            where = cols(chunk, BW, part * WIDTH)
            pairs.append((sink_ref.at[:, where], sinks.at[0:rows_s, where]))
        return [
            remote(src, dst, kv_s.at[i, chunk], kv_r.at[i, chunk], 1)
            for i, (src, dst) in enumerate(pairs)
        ]

    def q_copy(chunk, slot, index):
        return remote(
            q_ref.at[:, cols(chunk)], q_in.at[slot, :, cols(chunk)],
            q_s.at[slot, chunk], q_r.at[slot, chunk], index,
        )

    def sink_copy(which, index, own):
        where = pl.ds(which * rows_s, rows_s)
        src = sink_ref if own else sinks.at[where, :]
        return remote(src, sinks.at[where, :], s_s.at[which], s_r.at[which], index)

    def o_copy(chunk, slot, index):
        return remote(
            o_send.at[slot, :, cols(chunk)], o_recv.at[slot, :, cols(chunk)],
            o_s.at[slot, chunk], o_r.at[slot, chunk], index,
        )

    def st_copy(slot, index):
        return remote(st_send.at[slot], st_recv.at[slot], st_s.at[slot], st_r.at[slot], index)

    lanes = lax.broadcasted_iota(jnp.int32, st_send.shape[1:], 1)

    def partial(slot, chunk, pieces_of):
        stats = st_send[slot]
        for inner in range(BUNDLE):
            head = chunk * BUNDLE + inner
            blended, peak, total = attend(q_in[slot, :, head_cols(head)], pieces_of(head))
            o_send[slot, :, head_cols(head)] = blended.astype(jnp.bfloat16)
            stats = jnp.where(lanes == head, peak + jnp.log2(total), stats)
        st_send[slot] = stats

    def final(pieces_of, slots):
        def step(chunk, carry):
            for inner in range(BUNDLE):
                head = chunk * BUNDLE + inner
                where = head_cols(head)
                blended, peak, total = attend(q_ref[:, where], pieces_of(head))
                if slots:
                    levels = [peak + jnp.log2(total)]
                    outs = [blended]
                    for slot in slots:
                        levels.append(
                            jnp.sum(jnp.where(lanes == head, st_recv[slot], 0.0), axis=1, keepdims=True)
                        )
                        outs.append(o_recv[slot, :, where].astype(jnp.float32))
                    top = functools.reduce(jnp.maximum, levels)
                    shares = [jnp.exp2(level - top) for level in levels]
                    whole = functools.reduce(jnp.add, shares)
                    blended = functools.reduce(
                        jnp.add, [out * share for out, share in zip(outs, shares)]
                    ) / whole
                out_ref[:, where] = blended.astype(jnp.bfloat16)
            return carry
        lax.fori_loop(0, CHUNKS, step, 0)

    def pair(ref, head, low=None, high=None):
        rows = slice(low, high)
        return ref[rows, head_cols(head)], ref[rows, head_cols(head, WIDTH)]

    barrier = pltpu.get_barrier_semaphore()
    for step in range(1, WIN):
        pl.semaphore_signal(
            barrier, inc=1, device_id=at_place((place + step) % WIN), device_id_type=MESH
        )
    pl.semaphore_wait(barrier, WIN - 1)

    @pl.when(place == 0)
    def _():
        def send(chunk, carry):
            for copy in kv_copies(chunk):
                copy.start()
            return carry
        lax.fori_loop(0, CHUNKS, send, 0)
        sinks[0:rows_s, :] = sink_ref[...]
        for which in (1, 2, 3):
            sink_copy(which, 0, False).wait_recv()
        final(lambda head: [pair(sinks, head), pair(kv_ref, head)], ())

        def drain(chunk, carry):
            for copy in kv_copies(chunk):
                copy.wait_send()
            return carry
        lax.fori_loop(0, CHUNKS, drain, 0)

    @pl.when(place == 1)
    def _():
        sink_copy(1, 0, True).start()
        sinks[rows_s : 2 * rows_s, :] = sink_ref[...]
        st_send[...] = jnp.zeros_like(st_send)

        def work(chunk, carry):
            for copy in kv_copies(chunk):
                copy.wait_recv()
            for slot in range(2):
                q_copy(chunk, slot, 1).wait_recv()
                partial(
                    slot, chunk,
                    lambda head: [
                        pair(sinks, head, 0, 2 * rows_s), pair(kv_prev, head), pair(kv_ref, head)
                    ],
                )
                o_copy(chunk, slot, 2 + slot).start()
            return carry
        lax.fori_loop(0, CHUNKS - 2, work, 0)
        sink_copy(2, 1, False).wait_recv()
        sink_copy(2, 0, False).start()
        lax.fori_loop(CHUNKS - 2, CHUNKS - 1, work, 0)
        sink_copy(3, 1, False).wait_recv()
        sink_copy(3, 0, False).start()
        lax.fori_loop(CHUNKS - 1, CHUNKS, work, 0)
        for slot in range(2):
            st_copy(slot, 2 + slot).start()
        final(lambda head: [pair(sinks, head), pair(kv_prev, head), pair(kv_ref, head)], ())
        for which in (1, 2, 3):
            sink_copy(which, 0, which == 1).wait_send()

        def drain(chunk, carry):
            for slot in range(2):
                o_copy(chunk, slot, 2 + slot).wait_send()
            return carry
        lax.fori_loop(0, CHUNKS, drain, 0)
        for slot in range(2):
            st_copy(slot, 2 + slot).wait_send()

    @pl.when(place == 2)
    def _():
        for chunk in range(CHUNKS):
            if chunk == 2:
                sink_copy(2, 1, True).start()
            q_copy(chunk, 0, 1).start()
        sinks[2 * rows_s : 3 * rows_s, :] = sink_ref[...]
        st_send[0] = jnp.zeros_like(st_send[0])
        sink_copy(3, 2, False).wait_recv()
        sink_copy(3, 1, False).start()

        def work(chunk, carry):
            q_copy(chunk, 0, 2).wait_recv()
            partial(
                0, chunk,
                lambda head: [pair(sinks, head, 2 * rows_s, 3 * rows_s), pair(kv_ref, head)],
            )
            o_copy(chunk, 0, 3).start()
            return carry
        lax.fori_loop(0, CHUNKS, work, 0)
        st_copy(0, 3).start()

        def arrive(chunk, carry):
            o_copy(chunk, 0, 2).wait_recv()
            return carry
        lax.fori_loop(0, CHUNKS, arrive, 0)
        st_copy(0, 2).wait_recv()
        final(lambda head: [pair(sinks, head, 2 * rows_s, 4 * rows_s), pair(kv_ref, head)], (0,))
        sink_copy(2, 1, True).wait_send()
        sink_copy(3, 1, False).wait_send()

        def drain(chunk, carry):
            q_copy(chunk, 0, 1).wait_send()
            o_copy(chunk, 0, 3).wait_send()
            return carry
        lax.fori_loop(0, CHUNKS, drain, 0)
        st_copy(0, 3).wait_send()

    @pl.when(place == 3)
    def _():
        for chunk in range(CHUNKS):
            if chunk == 2:
                sink_copy(3, 2, True).start()
            q_copy(chunk, 1, 1).start()
        for chunk in range(CHUNKS):
            q_copy(chunk, 0, 2).start()

        def arrive(chunk, carry):
            for slot in range(2):
                o_copy(chunk, slot, 3).wait_recv()
            return carry
        lax.fori_loop(0, CHUNKS, arrive, 0)
        for slot in range(2):
            st_copy(slot, 3).wait_recv()
        final(lambda head: [pair(sink_ref, head), pair(kv_ref, head)], (0, 1))
        sink_copy(3, 2, True).wait_send()

        def drain(chunk, carry):
            q_copy(chunk, 1, 1).wait_send()
            q_copy(chunk, 0, 2).wait_send()
            return carry
        lax.fori_loop(0, CHUNKS, drain, 0)


def self_attention(queries, frame_kv, own_sink):
    rows = queries.shape[0]
    vmem = pl.BlockSpec(memory_space=pltpu.VMEM)
    dma = pltpu.SemaphoreType.DMA
    return pl.pallas_call(
        self_kernel,
        out_shape=jax.ShapeDtypeStruct((rows, WIDTH), jnp.bfloat16),
        in_specs=[vmem] * 3,
        out_specs=vmem,
        scratch_shapes=[
            pltpu.VMEM((rows, 2 * WIDTH), jnp.bfloat16),
            pltpu.VMEM((WIN * own_sink.shape[0], 2 * WIDTH), jnp.bfloat16),
            pltpu.VMEM((2, rows, WIDTH), jnp.bfloat16),
            pltpu.VMEM((2, rows, WIDTH), jnp.bfloat16),
            pltpu.VMEM((2, rows, WIDTH), jnp.bfloat16),
            pltpu.VMEM((2, rows, 128), jnp.float32),
            pltpu.VMEM((2, rows, 128), jnp.float32),
            dma((4, CHUNKS)), dma((4, CHUNKS)),
            dma((2, CHUNKS)), dma((2, CHUNKS)),
            dma((WIN,)), dma((WIN,)),
            dma((2, CHUNKS)), dma((2, CHUNKS)),
            dma((2,)), dma((2,)),
        ],
        compiler_params=pltpu.CompilerParams(
            collective_id=0, has_side_effects=True, vmem_limit_bytes=56 * 1024 * 1024
        ),
    )(queries, frame_kv, own_sink)


def cross_kernel(pick_ref, q_ref, k_ref, v_ref, out_ref):
    for inner in range(BUNDLE):
        where = slice(inner * HDIM, (inner + 1) * HDIM)
        blended, _, _ = attend(q_ref[:, where], [(k_ref[0, :, where], v_ref[0, :, where])])
        out_ref[:, where] = blended.astype(jnp.bfloat16)


def cross_attention(cross_queries, prompts, pick):
    rows = cross_queries.shape[0]
    tokens = prompts.shape[1]
    return pl.pallas_call(
        cross_kernel,
        out_shape=jax.ShapeDtypeStruct((rows, WIDTH), jnp.bfloat16),
        grid_spec=pltpu.PrefetchScalarGridSpec(
            num_scalar_prefetch=1,
            grid=(CHUNKS,),
            in_specs=[
                pl.BlockSpec((rows, BW), lambda c, pick: (0, c)),
                pl.BlockSpec((1, tokens, BW), lambda c, pick: (pick[0], 0, c)),
                pl.BlockSpec((1, tokens, BW), lambda c, pick: (pick[0], 0, CHUNKS + c)),
            ],
            out_specs=pl.BlockSpec((rows, BW), lambda c, pick: (0, c)),
        ),
    )(pick.reshape(1), cross_queries, prompts, prompts)


def shards(queries, cross_queries, frame_kv, sink_kv, prompt_kv, switch):
    stream_count = lax.axis_size("span") // WIN
    device = lax.axis_index("span")
    place = device // stream_count
    stream_of = device % stream_count
    stream_ids = jnp.arange(switch.shape[0], dtype=jnp.int32)
    switch_at = jnp.sum(jnp.where(stream_ids == stream_of, switch, 0))
    pick = (place >= switch_at).astype(jnp.int32)
    prompts = lax.all_gather(prompt_kv, "span", axis=1, tiled=True)
    own_sink = sink_kv.reshape(sink_kv.shape[1], sink_kv.shape[2])
    self_out = self_attention(queries, frame_kv, own_sink)
    cross_out = cross_attention(cross_queries, prompts, pick)
    return (self_out, cross_out)


def solution(mesh):
    in_specs = (
        P(("groups", "span"), None),
        P(("groups", "span"), None),
        P(("groups", "span"), None),
        P(("groups", "span"), None, None),
        P("groups", "span", None),
        P("groups"),
    )
    out_specs = (P(("groups", "span"), None), P(("groups", "span"), None))
    return jax.shard_map(shards, mesh=mesh, in_specs=in_specs, out_specs=out_specs, check_vma=False)
```

```python
import functools
import math

import jax
import jax.numpy as jnp
from jax import lax
from jax.experimental import pallas as pl
from jax.experimental.pallas import tpu as pltpu
from jax.sharding import PartitionSpec as P

HEADS = 20
HDIM = 128
WIN = 4
BUNDLE = 4
CHUNKS = HEADS // BUNDLE
BW = BUNDLE * HDIM
WIDTH = HEADS * HDIM
SCALE = 1.0 / math.sqrt(HDIM)
LOG2E = 1.4426950408889634
MESH = pl.DeviceIdType.MESH


def attend(query, pieces):
    scores = [
        lax.dot_general(query, keys, (((1,), (1,)), ((), ())), preferred_element_type=jnp.float32)
        for keys, _ in pieces
    ]
    peak = functools.reduce(
        jnp.maximum, [jnp.max(piece, axis=1, keepdims=True) for piece in scores]
    )
    total, blended = None, None
    for piece, (_, values) in zip(scores, pieces):
        weights = jnp.exp2((piece - peak) * (SCALE * LOG2E))
        part_sum = jnp.sum(weights, axis=1, keepdims=True)
        part = jnp.dot(weights.astype(jnp.bfloat16), values, preferred_element_type=jnp.float32)
        total = part_sum if total is None else total + part_sum
        blended = part if blended is None else blended + part
    return blended / total, peak * (SCALE * LOG2E), total


def cols(chunk, width=BW, base=0):
    return pl.ds(pl.multiple_of(base + chunk * width, 128), width)


def head_cols(head, base=0):
    return pl.ds(pl.multiple_of(base + head * HDIM, 128), HDIM)


def self_kernel(with_prompts, *refs):
    if with_prompts:
        (q_ref, kv_ref, sink_ref, prompt_ref, cq_ref, pick_ref, out_ref, cross_ref, *refs) = refs
        (bank, pr_s, pr_r, own_sem, *refs) = refs
    else:
        (q_ref, kv_ref, sink_ref, out_ref, *refs) = refs
    (kv_prev, sinks, q_in, o_send, o_recv, st_send, st_recv,
     kv_s, kv_r, q_s, q_r, s_s, s_r, o_s, o_r, st_s, st_r) = refs
    stride = lax.axis_size("span") // WIN
    me = lax.axis_index("span")
    place = me // stride
    stream = me % stride
    across = (stream + 2) % 4
    beside = stream + 1 - 2 * (stream % 2)
    rows_s = sink_ref.shape[0]
    rows = q_ref.shape[0]

    def at_place(index):
        return {"span": index * stride + stream}

    def remote(src, dst, send, recv, index, line=None):
        return pltpu.make_async_remote_copy(
            src_ref=src, dst_ref=dst, send_sem=send, recv_sem=recv,
            device_id=at_place(index) if line is None else {"span": index * stride + line},
            device_id_type=MESH,
        )

    def kv_copies(chunk):
        pairs = []
        for part in range(2):
            where = cols(chunk, BW, part * WIDTH)
            pairs.append((sink_ref.at[:, where], sinks.at[0:rows_s, where]))
        for part in range(2):
            where = cols(chunk, BW, part * WIDTH)
            pairs.append((kv_ref.at[:, where], kv_prev.at[:, where]))
        return [
            remote(src, dst, kv_s.at[i, chunk], kv_r.at[i, chunk], 1)
            for i, (src, dst) in enumerate(pairs)
        ]

    def q_copy(chunk, slot, index):
        return remote(
            q_ref.at[:, cols(chunk)], q_in.at[slot, :, cols(chunk)],
            q_s.at[slot, chunk], q_r.at[slot, chunk], index,
        )

    def sink_copy(which, index, own):
        where = pl.ds(which * rows_s, rows_s)
        src = sink_ref if own else sinks.at[where, :]
        return remote(src, sinks.at[where, :], s_s.at[which], s_r.at[which], index)

    def o_copy(chunk, slot, index):
        return remote(
            o_send.at[slot, :, cols(chunk)], o_recv.at[slot, :, cols(chunk)],
            o_s.at[slot, chunk], o_r.at[slot, chunk], index,
        )

    def st_copy(chunk, slot, index):
        return remote(
            st_send.at[slot, chunk], st_recv.at[slot, chunk],
            st_s.at[slot, chunk], st_r.at[slot, chunk], index,
        )

    def partial(slot, chunk, pieces_of, index):
        lanes = lax.broadcasted_iota(jnp.int32, (rows, 128), 1)
        stats = jnp.zeros((rows, 128), jnp.float32)
        for inner in range(BUNDLE):
            head = chunk * BUNDLE + inner
            blended, peak, total = attend(q_in[slot, :, head_cols(head)], pieces_of(head))
            o_send[slot, :, head_cols(head)] = blended.astype(jnp.bfloat16)
            stats = jnp.where(lanes == inner, peak + jnp.log2(total), stats)
        st_send[slot, chunk] = jnp.transpose(stats)[0:8]
        o_copy(chunk, slot, index).start()
        st_copy(chunk, slot, index).start()

    def drain_partial(slot, index):
        def drain(chunk, carry):
            o_copy(chunk, slot, index).wait_send()
            st_copy(chunk, slot, index).wait_send()
            return carry
        lax.fori_loop(0, CHUNKS, drain, 0)

    def final(chunk, pieces_of, slots, index):
        levels_in = []
        for slot in slots:
            o_copy(chunk, slot, index).wait_recv()
            st_copy(chunk, slot, index).wait_recv()
            padded = jnp.concatenate(
                [st_recv[slot, chunk], jnp.zeros((120, rows), jnp.float32)], axis=0
            )
            levels_in.append(jnp.transpose(padded))
        for inner in range(BUNDLE):
            where = head_cols(chunk * BUNDLE + inner)
            blended, peak, total = attend(q_ref[:, where], pieces_of(chunk * BUNDLE + inner))
            if slots:
                levels = [peak + jnp.log2(total)]
                outs = [blended]
                for slot, level in zip(slots, levels_in):
                    levels.append(level[:, inner : inner + 1])
                    outs.append(o_recv[slot, :, where].astype(jnp.float32))
                top = functools.reduce(jnp.maximum, levels)
                shares = [jnp.exp2(level - top) for level in levels]
                whole = functools.reduce(jnp.add, shares)
                blended = functools.reduce(
                    jnp.add, [out * share for out, share in zip(outs, shares)]
                ) / whole
            out_ref[:, where] = blended.astype(jnp.bfloat16)

    def loop(low, high, body):
        def step(chunk, carry):
            body(chunk)
            return carry
        lax.fori_loop(low, high, step, 0)

    def pair(ref, head, low=None, high=None):
        part = slice(low, high)
        return ref[part, head_cols(head)], ref[part, head_cols(head, WIDTH)]

    def prompt_copy(kind, piece, line, index, to_line, own=False):
        return remote(
            prompt_ref if own else bank.at[piece, line], bank.at[piece, line],
            pr_s.at[kind, piece], pr_r.at[kind if kind > 1 else 0, piece], index, to_line,
        )

    def line_copies(here, piece):
        own = here == piece
        copies = []
        if piece <= here < WIN - 1:
            copies.append(prompt_copy(0, piece, stream, here + 1, stream, own))
        if 0 < here <= piece:
            copies.append(prompt_copy(1, piece, stream, here - 1, stream, own))
        copies.append(prompt_copy(2, piece, stream, here, across, own))
        copies.append(prompt_copy(3, piece, stream, here, beside, own))
        return copies

    def own_copy(here):
        return pltpu.make_async_copy(prompt_ref, bank.at[here, stream], own_sem)

    def spread(here, piece):
        if not with_prompts:
            return
        if piece != here:
            prompt_copy(0, piece, stream, here, stream).wait_recv()
        for copy in line_copies(here, piece):
            copy.start()

    def spread_across(here, pieces):
        if not with_prompts:
            return
        for piece in pieces:
            prompt_copy(2, piece, across, here, stream).wait_recv()
            prompt_copy(4, piece, across, here, beside).start()

    def cross(here):
        if not with_prompts:
            return
        own_copy(here).wait()
        for piece in range(WIN):
            prompt_copy(3, piece, beside, here, stream).wait_recv()
            prompt_copy(4, piece, 3 - stream, here, stream).wait_recv()
        pick = pick_ref[0]
        tokens = bank.shape[0] * bank.shape[1] * bank.shape[3]

        def chunk_of(chunk):
            for inner in range(BUNDLE):
                head = chunk * BUNDLE + inner
                keys = bank[:, :, pick, :, head_cols(head)].reshape(tokens, HDIM)
                values = bank[:, :, pick, :, head_cols(head, WIDTH)].reshape(tokens, HDIM)
                blended, _, _ = attend(cq_ref[:, head_cols(head)], [(keys, values)])
                cross_ref[:, head_cols(head)] = blended.astype(jnp.bfloat16)
        loop(0, CHUNKS, chunk_of)

    def drain_prompts(here):
        if not with_prompts:
            return
        for piece in range(WIN):
            for copy in line_copies(here, piece):
                copy.wait_send()
            prompt_copy(4, piece, across, here, beside).wait_send()

    barrier = pltpu.get_barrier_semaphore()
    greeted = [at_place((place + step) % WIN) for step in range(1, WIN)]
    if with_prompts:
        greeted += [{"span": place * stride + across}, {"span": place * stride + beside}]
    for other in greeted:
        pl.semaphore_signal(barrier, inc=1, device_id=other, device_id_type=MESH)
    pl.semaphore_wait(barrier, len(greeted))

    @pl.when(place == 0)
    def _():
        spread(0, 0)

        def send(chunk):
            for copy in kv_copies(chunk):
                copy.start()
        loop(0, CHUNKS, send)
        if with_prompts:
            own_copy(0).start()
        sinks[0:rows_s, :] = sink_ref[...]
        spread(0, 1)
        spread(0, 2)
        spread(0, 3)
        spread_across(0, range(WIN))
        cross(0)
        for which in (1, 2, 3):
            sink_copy(which, 0, False).wait_recv()
        loop(0, CHUNKS, lambda chunk: final(
            chunk, lambda head: [pair(sinks, head), pair(kv_ref, head)], (), 0
        ))

        def drain(chunk):
            for copy in kv_copies(chunk):
                copy.wait_send()
        loop(0, CHUNKS, drain)
        drain_prompts(0)

    @pl.when(place == 1)
    def _():
        spread(1, 1)
        sink_copy(1, 0, True).start()
        if with_prompts:
            own_copy(1).start()
        sinks[rows_s : 2 * rows_s, :] = sink_ref[...]

        def work(chunk):
            for copy in kv_copies(chunk):
                copy.wait_recv()
            for slot in range(2):
                q_copy(chunk, slot, 1).wait_recv()
                partial(
                    slot, chunk,
                    lambda head: [
                        pair(sinks, head, 0, 2 * rows_s), pair(kv_prev, head), pair(kv_ref, head)
                    ],
                    2 + slot,
                )

        def ending(chunk):
            final(
                chunk, lambda head: [pair(sinks, head), pair(kv_prev, head), pair(kv_ref, head)], (), 1
            )
        spread(1, 0)
        spread(1, 2)
        loop(0, 1, work)
        spread(1, 3)
        loop(1, 2, work)
        sink_copy(3, 1, False).wait_recv()
        sink_copy(3, 0, False).start()
        loop(2, 3, work)
        sink_copy(2, 1, False).wait_recv()
        sink_copy(2, 0, False).start()
        spread_across(1, range(WIN))
        loop(3, CHUNKS - 1, work)
        cross(1)
        loop(0, CHUNKS - 1, ending)
        loop(CHUNKS - 1, CHUNKS, work)
        loop(CHUNKS - 1, CHUNKS, ending)
        for which in (1, 2, 3):
            sink_copy(which, 0, which == 1).wait_send()
        for slot in range(2):
            drain_partial(slot, 2 + slot)
        drain_prompts(1)

    @pl.when(place == 2)
    def _():
        spread(2, 2)
        q_copy(0, 0, 1).start()
        if with_prompts:
            own_copy(2).start()
        sinks[2 * rows_s : 3 * rows_s, :] = sink_ref[...]
        spread(2, 1)
        spread(2, 3)
        q_copy(1, 0, 1).start()
        spread(2, 0)
        sink_copy(3, 2, False).wait_recv()
        sink_copy(3, 1, False).start()
        q_copy(2, 0, 1).start()
        sink_copy(2, 1, True).start()
        loop(3, CHUNKS, lambda chunk: q_copy(chunk, 0, 1).start())
        spread_across(2, range(WIN))

        def work(chunk):
            q_copy(chunk, 0, 2).wait_recv()
            partial(
                0, chunk,
                lambda head: [pair(sinks, head, 2 * rows_s, 3 * rows_s), pair(kv_ref, head)], 3,
            )
        cross(2)
        loop(0, CHUNKS, work)
        loop(0, CHUNKS, lambda chunk: final(
            chunk, lambda head: [pair(sinks, head, 2 * rows_s, 4 * rows_s), pair(kv_ref, head)], (0,), 2
        ))
        sink_copy(2, 1, True).wait_send()
        sink_copy(3, 1, False).wait_send()
        loop(0, CHUNKS, lambda chunk: q_copy(chunk, 0, 1).wait_send())
        drain_partial(0, 3)
        drain_prompts(2)

    @pl.when(place == 3)
    def _():
        spread(3, 3)
        sink_copy(3, 2, True).start()
        loop(0, CHUNKS, lambda chunk: q_copy(chunk, 1, 1).start())
        loop(0, CHUNKS, lambda chunk: q_copy(chunk, 0, 2).start())
        if with_prompts:
            own_copy(3).start()
        spread(3, 2)
        spread(3, 1)
        spread(3, 0)
        spread_across(3, range(WIN - 1, -1, -1))
        cross(3)
        loop(0, CHUNKS, lambda chunk: final(
            chunk, lambda head: [pair(sink_ref, head), pair(kv_ref, head)], (0, 1), 3
        ))
        sink_copy(3, 2, True).wait_send()
        loop(0, CHUNKS, lambda chunk: q_copy(chunk, 1, 1).wait_send())
        loop(0, CHUNKS, lambda chunk: q_copy(chunk, 0, 2).wait_send())
        drain_prompts(3)


def self_attention(queries, frame_kv, own_sink, prompts=None):
    rows = queries.shape[0]
    vmem = pl.BlockSpec(memory_space=pltpu.VMEM)
    dma = pltpu.SemaphoreType.DMA
    operands = [queries, frame_kv, own_sink]
    in_specs = [vmem] * 3
    outs = [jax.ShapeDtypeStruct((rows, WIDTH), jnp.bfloat16)]
    scratch = []
    if prompts is not None:
        operands += prompts
        in_specs += [vmem, vmem, pl.BlockSpec(memory_space=pltpu.SMEM)]
        outs = outs * 2
        scratch = [
            pltpu.VMEM((WIN, lax.axis_size("span") // WIN) + prompts[0].shape, jnp.bfloat16),
            dma((5, WIN)), dma((5, WIN)), dma,
        ]
    return pl.pallas_call(
        functools.partial(self_kernel, prompts is not None),
        out_shape=outs,
        in_specs=in_specs,
        out_specs=[vmem] * len(outs),
        scratch_shapes=scratch + [
            pltpu.VMEM((rows, 2 * WIDTH), jnp.bfloat16),
            pltpu.VMEM((WIN * own_sink.shape[0], 2 * WIDTH), jnp.bfloat16),
            pltpu.VMEM((2, rows, WIDTH), jnp.bfloat16),
            pltpu.VMEM((2, rows, WIDTH), jnp.bfloat16),
            pltpu.VMEM((2, rows, WIDTH), jnp.bfloat16),
            pltpu.VMEM((2, CHUNKS, 8, rows), jnp.float32),
            pltpu.VMEM((2, CHUNKS, 8, rows), jnp.float32),
            dma((4, CHUNKS)), dma((4, CHUNKS)),
            dma((2, CHUNKS)), dma((2, CHUNKS)),
            dma((WIN,)), dma((WIN,)),
            dma((2, CHUNKS)), dma((2, CHUNKS)),
            dma((2, CHUNKS)), dma((2, CHUNKS)),
        ],
        compiler_params=pltpu.CompilerParams(
            collective_id=0, has_side_effects=True, vmem_limit_bytes=60 * 1024 * 1024
        ),
    )(*operands)


def cross_kernel(pick_ref, q_ref, k_ref, v_ref, out_ref):
    for inner in range(BUNDLE):
        where = slice(inner * HDIM, (inner + 1) * HDIM)
        blended, _, _ = attend(q_ref[:, where], [(k_ref[0, :, where], v_ref[0, :, where])])
        out_ref[:, where] = blended.astype(jnp.bfloat16)


def cross_attention(cross_queries, prompts, pick):
    rows = cross_queries.shape[0]
    tokens = prompts.shape[1]
    return pl.pallas_call(
        cross_kernel,
        out_shape=jax.ShapeDtypeStruct((rows, WIDTH), jnp.bfloat16),
        grid_spec=pltpu.PrefetchScalarGridSpec(
            num_scalar_prefetch=1,
            grid=(CHUNKS,),
            in_specs=[
                pl.BlockSpec((rows, BW), lambda c, pick: (0, c)),
                pl.BlockSpec((1, tokens, BW), lambda c, pick: (pick[0], 0, c)),
                pl.BlockSpec((1, tokens, BW), lambda c, pick: (pick[0], 0, CHUNKS + c)),
            ],
            out_specs=pl.BlockSpec((rows, BW), lambda c, pick: (0, c)),
        ),
    )(pick.reshape(1), cross_queries, prompts, prompts)


def shards(queries, cross_queries, frame_kv, sink_kv, prompt_kv, switch):
    stream_count = lax.axis_size("span") // WIN
    device = lax.axis_index("span")
    place = device // stream_count
    stream_of = device % stream_count
    stream_ids = jnp.arange(switch.shape[0], dtype=jnp.int32)
    switch_at = jnp.sum(jnp.where(stream_ids == stream_of, switch, 0))
    pick = (place >= switch_at).astype(jnp.int32)
    own_sink = sink_kv.reshape(sink_kv.shape[1], sink_kv.shape[2])
    if stream_count == 4 and prompt_kv.shape[1] % 16 == 0:
        return tuple(
            self_attention(queries, frame_kv, own_sink, [prompt_kv, cross_queries, pick.reshape(1)])
        )
    prompts = lax.all_gather(prompt_kv, "span", axis=1, tiled=True)
    (self_out,) = self_attention(queries, frame_kv, own_sink)
    cross_out = cross_attention(cross_queries, prompts, pick)
    return (self_out, cross_out)


def solution(mesh):
    in_specs = (
        P(("groups", "span"), None),
        P(("groups", "span"), None),
        P(("groups", "span"), None),
        P(("groups", "span"), None, None),
        P("groups", "span", None),
        P("groups"),
    )
    out_specs = (P(("groups", "span"), None), P(("groups", "span"), None))
    return jax.shard_map(shards, mesh=mesh, in_specs=in_specs, out_specs=out_specs, check_vma=False)
```

```python
import functools
import math

import jax
import jax.numpy as jnp
from jax import lax
from jax.experimental import pallas as pl
from jax.experimental.pallas import tpu as pltpu
from jax.sharding import PartitionSpec as P

HEADS = 20
HDIM = 128
WIN = 4
BUNDLE = 4
CHUNKS = HEADS // BUNDLE
BW = BUNDLE * HDIM
WIDTH = HEADS * HDIM
SCALE = 1.0 / math.sqrt(HDIM)
LOG2E = 1.4426950408889634
MESH = pl.DeviceIdType.MESH


def attend(query, pieces):
    scores = [
        lax.dot_general(query, keys, (((1,), (1,)), ((), ())), preferred_element_type=jnp.float32)
        for keys, _ in pieces
    ]
    peak = functools.reduce(
        jnp.maximum, [jnp.max(piece, axis=1, keepdims=True) for piece in scores]
    )
    total, blended = None, None
    for piece, (_, values) in zip(scores, pieces):
        weights = jnp.exp2((piece - peak) * (SCALE * LOG2E))
        part_sum = jnp.sum(weights, axis=1, keepdims=True)
        part = jnp.dot(weights.astype(jnp.bfloat16), values, preferred_element_type=jnp.float32)
        total = part_sum if total is None else total + part_sum
        blended = part if blended is None else blended + part
    return blended / total, peak * (SCALE * LOG2E), total


def cols(chunk, width=BW, base=0):
    return pl.ds(pl.multiple_of(base + chunk * width, 128), width)


def head_cols(head, base=0):
    return pl.ds(pl.multiple_of(base + head * HDIM, 128), HDIM)


def self_kernel(with_prompts, *refs):
    if with_prompts:
        (q_ref, kv_ref, sink_ref, prompt_ref, cq_ref, pick_ref, out_ref, cross_ref, *refs) = refs
        (bank, pr_s, pr_r, own_sem, *refs) = refs
    else:
        (q_ref, kv_ref, sink_ref, out_ref, *refs) = refs
    (kv_prev, sinks, q_in, o_send, o_recv, st_send, st_recv,
     kv_s, kv_r, q_s, q_r, s_s, s_r, o_s, o_r, st_s, st_r) = refs
    stride = lax.axis_size("span") // WIN
    me = lax.axis_index("span")
    place = me // stride
    stream = me % stride
    across = (stream + 2) % 4
    beside = stream + 1 - 2 * (stream % 2)
    rows_s = sink_ref.shape[0]
    rows = q_ref.shape[0]

    def at_place(index):
        return {"span": index * stride + stream}

    def remote(src, dst, send, recv, index, line=None):
        return pltpu.make_async_remote_copy(
            src_ref=src, dst_ref=dst, send_sem=send, recv_sem=recv,
            device_id=at_place(index) if line is None else {"span": index * stride + line},
            device_id_type=MESH,
        )

    def kv_copies(chunk):
        pairs = []
        for part in range(2):
            where = cols(chunk, BW, part * WIDTH)
            pairs.append((sink_ref.at[:, where], sinks.at[0:rows_s, where]))
        for part in range(2):
            where = cols(chunk, BW, part * WIDTH)
            pairs.append((kv_ref.at[:, where], kv_prev.at[:, where]))
        return [
            remote(src, dst, kv_s.at[i, chunk], kv_r.at[i, chunk], 1)
            for i, (src, dst) in enumerate(pairs)
        ]

    def q_copy(chunk, slot, index):
        return remote(
            q_ref.at[:, cols(chunk)], q_in.at[slot, :, cols(chunk)],
            q_s.at[slot, chunk], q_r.at[slot, chunk], index,
        )

    def q_relay(chunk):
        return remote(
            q_in.at[0, :, cols(chunk)], q_in.at[1, :, cols(chunk)],
            q_s.at[1, chunk], q_r.at[1, chunk], 1,
        )

    def sink_copy(which, index, own):
        where = pl.ds(which * rows_s, rows_s)
        src = sink_ref if own else sinks.at[where, :]
        return remote(src, sinks.at[where, :], s_s.at[which], s_r.at[which], index)

    def o_copy(chunk, slot, index):
        return remote(
            o_send.at[slot, :, cols(chunk)], o_recv.at[slot, :, cols(chunk)],
            o_s.at[slot, chunk], o_r.at[slot, chunk], index,
        )

    def st_copy(chunk, slot, index):
        return remote(
            st_send.at[slot, chunk], st_recv.at[slot, chunk],
            st_s.at[slot, chunk], st_r.at[slot, chunk], index,
        )

    def partial(slot, chunk, pieces_of, index):
        lanes = lax.broadcasted_iota(jnp.int32, (rows, 128), 1)
        stats = jnp.zeros((rows, 128), jnp.float32)
        for inner in range(BUNDLE):
            head = chunk * BUNDLE + inner
            blended, peak, total = attend(q_in[slot, :, head_cols(head)], pieces_of(head))
            o_send[slot, :, head_cols(head)] = blended.astype(jnp.bfloat16)
            stats = jnp.where(lanes == inner, peak + jnp.log2(total), stats)
        st_send[slot, chunk] = jnp.transpose(stats)[0:8]
        o_copy(chunk, slot, index).start()
        st_copy(chunk, slot, index).start()

    def drain_partial(slot, index):
        def drain(chunk, carry):
            o_copy(chunk, slot, index).wait_send()
            st_copy(chunk, slot, index).wait_send()
            return carry
        lax.fori_loop(0, CHUNKS, drain, 0)

    def final(chunk, pieces_of, slots, index):
        levels_in = []
        for slot in slots:
            o_copy(chunk, slot, index).wait_recv()
            st_copy(chunk, slot, index).wait_recv()
            padded = jnp.concatenate(
                [st_recv[slot, chunk], jnp.zeros((120, rows), jnp.float32)], axis=0
            )
            levels_in.append(jnp.transpose(padded))
        for inner in range(BUNDLE):
            where = head_cols(chunk * BUNDLE + inner)
            blended, peak, total = attend(q_ref[:, where], pieces_of(chunk * BUNDLE + inner))
            if slots:
                levels = [peak + jnp.log2(total)]
                outs = [blended]
                for slot, level in zip(slots, levels_in):
                    levels.append(level[:, inner : inner + 1])
                    outs.append(o_recv[slot, :, where].astype(jnp.float32))
                top = functools.reduce(jnp.maximum, levels)
                shares = [jnp.exp2(level - top) for level in levels]
                whole = functools.reduce(jnp.add, shares)
                blended = functools.reduce(
                    jnp.add, [out * share for out, share in zip(outs, shares)]
                ) / whole
            out_ref[:, where] = blended.astype(jnp.bfloat16)

    def loop(low, high, body):
        def step(chunk, carry):
            body(chunk)
            return carry
        lax.fori_loop(low, high, step, 0)

    def pair(ref, head, low=None, high=None):
        part = slice(low, high)
        return ref[part, head_cols(head)], ref[part, head_cols(head, WIDTH)]

    def prompt_copy(kind, piece, line, index, to_line, own=False):
        return remote(
            prompt_ref if own else bank.at[piece, line], bank.at[piece, line],
            pr_s.at[kind, piece], pr_r.at[kind if kind > 1 else 0, piece], index, to_line,
        )

    def line_copies(here, piece):
        own = here == piece
        copies = []
        if piece <= here < WIN - 1:
            copies.append(prompt_copy(0, piece, stream, here + 1, stream, own))
        if 0 < here <= piece:
            copies.append(prompt_copy(1, piece, stream, here - 1, stream, own))
        copies.append(prompt_copy(2, piece, stream, here, across, own))
        copies.append(prompt_copy(3, piece, stream, here, beside, own))
        return copies

    def own_copy(here):
        return pltpu.make_async_copy(prompt_ref, bank.at[here, stream], own_sem)

    def spread(here, piece):
        if not with_prompts:
            return
        if piece != here:
            prompt_copy(0, piece, stream, here, stream).wait_recv()
        for copy in line_copies(here, piece):
            copy.start()

    def spread_across(here, pieces):
        if not with_prompts:
            return
        for piece in pieces:
            prompt_copy(2, piece, across, here, stream).wait_recv()
            prompt_copy(4, piece, across, here, beside).start()

    def cross(here):
        if not with_prompts:
            return
        own_copy(here).wait()
        for piece in range(WIN):
            prompt_copy(3, piece, beside, here, stream).wait_recv()
            prompt_copy(4, piece, 3 - stream, here, stream).wait_recv()
        pick = (place >= pick_ref[stream]).astype(jnp.int32)
        tokens = bank.shape[0] * bank.shape[1] * bank.shape[3]

        def chunk_of(chunk):
            for inner in range(BUNDLE):
                head = chunk * BUNDLE + inner
                keys = bank[:, :, pick, :, head_cols(head)].reshape(tokens, HDIM)
                values = bank[:, :, pick, :, head_cols(head, WIDTH)].reshape(tokens, HDIM)
                blended, _, _ = attend(cq_ref[:, head_cols(head)], [(keys, values)])
                cross_ref[:, head_cols(head)] = blended.astype(jnp.bfloat16)
        loop(0, CHUNKS, chunk_of)

    def drain_prompts(here):
        if not with_prompts:
            return
        for piece in range(WIN):
            for copy in line_copies(here, piece):
                copy.wait_send()
            prompt_copy(4, piece, across, here, beside).wait_send()

    barrier = pltpu.get_barrier_semaphore()
    greeted = [at_place((place + step) % WIN) for step in range(1, WIN)]
    if with_prompts:
        greeted += [{"span": place * stride + across}, {"span": place * stride + beside}]
    for other in greeted:
        pl.semaphore_signal(barrier, inc=1, device_id=other, device_id_type=MESH)
    pl.semaphore_wait(barrier, len(greeted))

    @pl.when(place == 0)
    def _():
        spread(0, 0)

        def send(chunk):
            for copy in kv_copies(chunk):
                copy.start()
        loop(0, CHUNKS, send)
        if with_prompts:
            own_copy(0).start()
        sinks[0:rows_s, :] = sink_ref[...]
        spread(0, 1)
        spread(0, 2)
        spread(0, 3)
        spread_across(0, range(WIN))
        cross(0)
        for which in (1, 2, 3):
            sink_copy(which, 0, False).wait_recv()
        loop(0, CHUNKS, lambda chunk: final(
            chunk, lambda head: [pair(sinks, head), pair(kv_ref, head)], (), 0
        ))

        def drain(chunk):
            for copy in kv_copies(chunk):
                copy.wait_send()
        loop(0, CHUNKS, drain)
        drain_prompts(0)

    @pl.when(place == 1)
    def _():
        spread(1, 1)
        sink_copy(1, 0, True).start()
        if with_prompts:
            own_copy(1).start()
        sinks[rows_s : 2 * rows_s, :] = sink_ref[...]

        def work(chunk):
            for copy in kv_copies(chunk):
                copy.wait_recv()
            for slot in range(2):
                q_copy(chunk, slot, 1).wait_recv()
                partial(
                    slot, chunk,
                    lambda head: [
                        pair(sinks, head, 0, 2 * rows_s), pair(kv_prev, head), pair(kv_ref, head)
                    ],
                    2 + slot,
                )

        def ending(chunk):
            final(
                chunk, lambda head: [pair(sinks, head), pair(kv_prev, head), pair(kv_ref, head)], (), 1
            )
        spread(1, 0)
        spread(1, 2)
        spread(1, 3)
        loop(0, 2, work)
        sink_copy(3, 1, False).wait_recv()
        sink_copy(3, 0, False).start()
        spread_across(1, range(WIN))
        sink_copy(2, 1, False).wait_recv()
        sink_copy(2, 0, False).start()
        cross(1)
        loop(0, 2, ending)

        def both(chunk):
            work(chunk)
            ending(chunk)
        loop(2, CHUNKS, both)
        for which in (1, 2, 3):
            sink_copy(which, 0, which == 1).wait_send()
        for slot in range(2):
            drain_partial(slot, 2 + slot)
        drain_prompts(1)

    @pl.when(place == 2)
    def _():
        spread(2, 2)
        q_copy(0, 0, 1).start()
        if with_prompts:
            own_copy(2).start()
        sinks[2 * rows_s : 3 * rows_s, :] = sink_ref[...]
        spread(2, 3)
        spread(2, 1)

        def relay(chunk):
            q_copy(chunk, 0, 2).wait_recv()
            q_relay(chunk).start()
        relay(0)
        q_copy(1, 0, 1).start()
        relay(1)
        spread(2, 0)
        sink_copy(3, 2, False).wait_recv()
        sink_copy(3, 1, False).start()
        sink_copy(2, 1, True).start()

        def send(chunk):
            q_copy(chunk, 0, 1).start()
            relay(chunk)
        loop(2, CHUNKS, send)
        spread_across(2, range(WIN))

        def work(chunk):
            partial(
                0, chunk,
                lambda head: [pair(sinks, head, 2 * rows_s, 3 * rows_s), pair(kv_ref, head)], 3,
            )
        cross(2)
        loop(0, CHUNKS, work)
        loop(0, CHUNKS, lambda chunk: final(
            chunk, lambda head: [pair(sinks, head, 2 * rows_s, 4 * rows_s), pair(kv_ref, head)], (0,), 2
        ))
        sink_copy(2, 1, True).wait_send()
        sink_copy(3, 1, False).wait_send()
        loop(0, CHUNKS, lambda chunk: q_copy(chunk, 0, 1).wait_send())
        loop(0, CHUNKS, lambda chunk: q_relay(chunk).wait_send())
        drain_partial(0, 3)
        drain_prompts(2)

    @pl.when(place == 3)
    def _():
        spread(3, 3)
        loop(0, 2, lambda chunk: q_copy(chunk, 0, 2).start())
        sink_copy(3, 2, True).start()
        loop(2, CHUNKS, lambda chunk: q_copy(chunk, 0, 2).start())
        if with_prompts:
            own_copy(3).start()
        spread(3, 2)
        spread(3, 1)
        spread(3, 0)
        spread_across(3, range(WIN - 1, -1, -1))
        cross(3)
        loop(0, CHUNKS, lambda chunk: final(
            chunk, lambda head: [pair(sink_ref, head), pair(kv_ref, head)], (0, 1), 3
        ))
        sink_copy(3, 2, True).wait_send()
        loop(0, CHUNKS, lambda chunk: q_copy(chunk, 0, 2).wait_send())
        drain_prompts(3)


def self_attention(queries, frame_kv, own_sink, prompts=None):
    rows = queries.shape[0]
    vmem = pl.BlockSpec(memory_space=pltpu.VMEM)
    dma = pltpu.SemaphoreType.DMA
    operands = [queries, frame_kv, own_sink]
    in_specs = [vmem] * 3
    outs = [jax.ShapeDtypeStruct((rows, WIDTH), jnp.bfloat16)]
    scratch = []
    if prompts is not None:
        operands += prompts
        in_specs += [vmem, vmem, pl.BlockSpec(memory_space=pltpu.SMEM)]
        outs = outs * 2
        scratch = [
            pltpu.VMEM((WIN, lax.axis_size("span") // WIN) + prompts[0].shape, jnp.bfloat16),
            dma((5, WIN)), dma((5, WIN)), dma,
        ]
    return pl.pallas_call(
        functools.partial(self_kernel, prompts is not None),
        out_shape=outs,
        in_specs=in_specs,
        out_specs=[vmem] * len(outs),
        scratch_shapes=scratch + [
            pltpu.VMEM((rows, 2 * WIDTH), jnp.bfloat16),
            pltpu.VMEM((WIN * own_sink.shape[0], 2 * WIDTH), jnp.bfloat16),
            pltpu.VMEM((2, rows, WIDTH), jnp.bfloat16),
            pltpu.VMEM((2, rows, WIDTH), jnp.bfloat16),
            pltpu.VMEM((2, rows, WIDTH), jnp.bfloat16),
            pltpu.VMEM((2, CHUNKS, 8, rows), jnp.float32),
            pltpu.VMEM((2, CHUNKS, 8, rows), jnp.float32),
            dma((4, CHUNKS)), dma((4, CHUNKS)),
            dma((2, CHUNKS)), dma((2, CHUNKS)),
            dma((WIN,)), dma((WIN,)),
            dma((2, CHUNKS)), dma((2, CHUNKS)),
            dma((2, CHUNKS)), dma((2, CHUNKS)),
        ],
        compiler_params=pltpu.CompilerParams(
            collective_id=0, has_side_effects=True, vmem_limit_bytes=60 * 1024 * 1024
        ),
    )(*operands)


def cross_kernel(pick_ref, q_ref, k_ref, v_ref, out_ref):
    for inner in range(BUNDLE):
        where = slice(inner * HDIM, (inner + 1) * HDIM)
        blended, _, _ = attend(q_ref[:, where], [(k_ref[0, :, where], v_ref[0, :, where])])
        out_ref[:, where] = blended.astype(jnp.bfloat16)


def cross_attention(cross_queries, prompts, pick):
    rows = cross_queries.shape[0]
    tokens = prompts.shape[1]
    return pl.pallas_call(
        cross_kernel,
        out_shape=jax.ShapeDtypeStruct((rows, WIDTH), jnp.bfloat16),
        grid_spec=pltpu.PrefetchScalarGridSpec(
            num_scalar_prefetch=1,
            grid=(CHUNKS,),
            in_specs=[
                pl.BlockSpec((rows, BW), lambda c, pick: (0, c)),
                pl.BlockSpec((1, tokens, BW), lambda c, pick: (pick[0], 0, c)),
                pl.BlockSpec((1, tokens, BW), lambda c, pick: (pick[0], 0, CHUNKS + c)),
            ],
            out_specs=pl.BlockSpec((rows, BW), lambda c, pick: (0, c)),
        ),
    )(pick.reshape(1), cross_queries, prompts, prompts)


def shards(queries, cross_queries, frame_kv, sink_kv, prompt_kv, switch):
    stream_count = lax.axis_size("span") // WIN
    device = lax.axis_index("span")
    place = device // stream_count
    stream_of = device % stream_count
    own_sink = sink_kv.reshape(sink_kv.shape[1], sink_kv.shape[2])
    if stream_count == 4 and prompt_kv.shape[1] % 16 == 0:
        return tuple(
            self_attention(queries, frame_kv, own_sink, [prompt_kv, cross_queries, switch])
        )
    stream_ids = jnp.arange(switch.shape[0], dtype=jnp.int32)
    switch_at = jnp.sum(jnp.where(stream_ids == stream_of, switch, 0))
    pick = (place >= switch_at).astype(jnp.int32)
    prompts = lax.all_gather(prompt_kv, "span", axis=1, tiled=True)
    (self_out,) = self_attention(queries, frame_kv, own_sink)
    cross_out = cross_attention(cross_queries, prompts, pick)
    return (self_out, cross_out)


def solution(mesh):
    in_specs = (
        P(("groups", "span"), None),
        P(("groups", "span"), None),
        P(("groups", "span"), None),
        P(("groups", "span"), None, None),
        P("groups", "span", None),
        P("groups"),
    )
    out_specs = (P(("groups", "span"), None), P(("groups", "span"), None))
    return jax.shard_map(shards, mesh=mesh, in_specs=in_specs, out_specs=out_specs, check_vma=False)
```
